512 devices in a mesh: dp: 16 (over x, y_hi), dom: 32 (over z, y_lo, core).
Axes of the slice: x: 4, y: 8 (y_hi: 4, y_lo: 2; y = y_hi * 2 + y_lo), z: 8, core: 2. Of those that a mesh axis runs over, the one named last changes fastest.
Arguments:
- features: bfloat16 [16, 16384, 128], P('dp', 'dom'), may hold values from -6 to 6
- keep_masks: bfloat16 [16, 4, 16384], P('dp', None, 'dom'), may hold values from 0 to 1, as said below
- serve_ids: int32 [16, 32, 32, 1], P('dp', 'dom'), may hold values from 0 to 3, as said below
- col_slot: int32 [16, 128, 10], P('dp', 'dom'), may hold values from 0 to 35, as said below
- adj_blocks: bfloat16 [16, 128, 10, 128, 128], P('dp', 'dom'), may hold values from -0.15625 to 0.15625
- node_labels: int32 [16, 16384], P('dp', 'dom'), may hold values from 0 to 171
- labeled: int32 [16, 16384], P('dp', 'dom'), may hold values 0 or 1
- weight_in: bfloat16 [128, 1024], replicated, may hold values from -0.5 to 0.5
- bias_in: float32 [1024], replicated, may hold values from -3 to 3
- weight_out: bfloat16 [1024, 172], replicated, may hold values from -0.1875 to 0.1875
- bias_out: float32 [172], replicated, may hold values from -4 to 4
Outputs:
- grad_weight_in: float32 [128, 1024], replicated
- grad_bias_in: float32 [1024], replicated
- grad_weight_out: float32 [1024, 172], replicated
- grad_bias_out: float32 [172], replicated
The draws below stay inside these ranges and needn't reach their ends.
Inputs may be any that keep to these rules, and one draw needn't show every extreme that they name: `serve_ids`: for each batch, sending device and receiving device: 1 distinct own tile numbers of the sender. `col_slot`: slots below 32 name received tiles; within one device's row tiles every such slot is named exactly once and each own tile slot exactly 2 times. `keep_masks`: values are 0 or 1.
All inputs are finite; a program needn't handle non-finite values. No bound on the sum of `labeled` on one device may be relied on, other than what follows from the above.
Results may differ from the reference program's by a relative error of at most 0.0015.
Values may be sent and summed in bfloat16 or wider, within the bound.
A program may use at most 64 MiB of HBM per device.

```python
import jax
import jax.numpy as jnp
from jax import lax

FEAT = 128
CLASSES = 172
HIDDEN_SIZE = 1024
TILE = 128
SAMPLES = 4
ORDER = 2
CAP = 1
LOCAL = 2
TILES_DEV = 4
NB = 16
NODE_DEV = 512
TILES = 128
NODES = 16384
NNZ = 10
N_DOM = 32


def draw_keep_masks(key, part):
    return jax.random.randint(key, (NB, SAMPLES, NODES), 0, 2).astype(jnp.float32).astype(jnp.bfloat16)


def draw_serve_ids(key, part):
    subkeys = jax.random.split(key, NB * N_DOM * N_DOM)

    def choose(subkey):
        return jax.random.permutation(subkey, TILES_DEV)[:CAP]
    chosen = jax.vmap(choose)(subkeys)
    return chosen.reshape(NB, N_DOM, N_DOM, CAP).astype(jnp.int32)


def draw_col_slot(key, part):
    remote = N_DOM * CAP
    slot_list = jnp.concatenate([jnp.arange(remote, dtype=jnp.int32), remote + jnp.repeat(jnp.arange(TILES_DEV, dtype=jnp.int32), LOCAL)])
    subkeys = jax.random.split(key, NB * N_DOM)

    def shuffle(subkey):
        return jax.random.permutation(subkey, slot_list)
    shuffled = jax.vmap(shuffle)(subkeys)
    return shuffled.reshape(NB, TILES, NNZ).astype(jnp.int32)


def plant(drawn, key, smallest, top_value):
    index_at = [jax.random.randint(jax.random.fold_in(key, axis), (), 0, length) for axis, length in enumerate(drawn.shape)]
    main_axis = drawn.shape.index(max(drawn.shape))
    next_to = index_at[:main_axis] + [(index_at[main_axis] + 1) % drawn.shape[main_axis]] + index_at[main_axis + 1:]
    return drawn.at[tuple(index_at)].set(smallest).at[tuple(next_to)].set(top_value)


def shard_levels(stream_key, dims, shards, least, high):
    loudness, own = 1.0, jax.random.fold_in(stream_key, 6)
    for axis_at, blocks in shards:
        draws = jnp.exp(jax.random.uniform(jax.random.fold_in(own, axis_at), (blocks,), jnp.float32, least / len(shards), high / len(shards)))
        loudness = loudness * jnp.repeat(draws, dims[axis_at] // blocks).reshape([-1 if axis == axis_at else 1 for axis in range(len(dims))])
    return loudness


def gaussian(rng, dims, spread, most, cuts=(), held_as=jnp.bfloat16):
    factor_of = shard_levels(rng, dims, cuts, -0.22, 0.18) if cuts else 1.0
    values = jax.random.normal(rng, dims, jnp.float32) * spread * factor_of
    return jnp.minimum(jnp.maximum(values, -most), most).astype(held_as)


def setup_inputs(seed: int = 0) -> dict:
    keys = jax.random.split(jax.random.key(seed), 12)
    features = gaussian(keys[0], (NB, NODES, FEAT), 1.0, 6.0, ((0, 16), (1, 32)))
    keep_masks = draw_keep_masks(jax.random.fold_in(keys[11], 71), 0)
    serve_ids = draw_serve_ids(jax.random.fold_in(keys[11], 71), 0)
    col_slot = draw_col_slot(jax.random.fold_in(keys[11], 71), 0)
    adj_blocks = gaussian(keys[4], (NB, TILES, NNZ, TILE, TILE), (TILE * NNZ) ** -0.5, 0.15625, ((0, 16), (1, 32)))
    node_labels = plant(jax.random.randint(keys[5], (NB, NODES), 0, CLASSES), jax.random.fold_in(keys[5], 1), 0, CLASSES - 1).astype(jnp.int32)
    labeled = plant((jax.random.randint(keys[6], (NB, NODES), 0, 2) < 1).astype(jnp.int32), jax.random.fold_in(keys[6], 1), 0, 1)
    weight_in = gaussian(keys[7], (FEAT, HIDDEN_SIZE), FEAT ** -0.5, 0.5)
    bias_in = gaussian(keys[8], (HIDDEN_SIZE,), 0.5, 3.0, (), jnp.float32)
    weight_out = gaussian(keys[9], (HIDDEN_SIZE, CLASSES), HIDDEN_SIZE ** -0.5, 0.1875)
    bias_out = gaussian(keys[10], (CLASSES,), 1.0, 4.0, (), jnp.float32)
    return dict(features=features, keep_masks=keep_masks, serve_ids=serve_ids, col_slot=col_slot, adj_blocks=adj_blocks, node_labels=node_labels, labeled=labeled, weight_in=weight_in, bias_in=bias_in, weight_out=weight_out, bias_out=bias_out)


KEEP_RATE = 0.5


def column_tiles(serve_ids, col_slot):
    remote = N_DOM * CAP
    requester = (jnp.arange(TILES, dtype=jnp.int32) // TILES_DEV)[:, None]
    clipped = jnp.minimum(col_slot, remote - 1).astype(jnp.int32)
    sender = clipped // CAP
    which_one = clipped % CAP
    served = serve_ids[sender, requester, which_one]
    far_tile = sender * TILES_DEV + served
    near_tile = requester * TILES_DEV + (col_slot - remote)
    return jnp.where(col_slot < remote, far_tile, near_tile).astype(jnp.int32)


def propagate(current, adj_blocks, columns):
    def one_tile(pair):
        tile_blocks, tile_cols = pair
        picked = current[tile_cols].astype(jnp.float32)
        return jnp.einsum("jab,jsbf->saf", tile_blocks.astype(jnp.float32), picked)
    return lax.map(one_tile, (adj_blocks, columns))


def mlp_grads(xbar, node_labels, labeled, weight_in, bias_in, weight_out, bias_out, scale):
    row_tiles, samples, tile_size, feat_size = xbar.shape
    classes = weight_out.shape[1]
    node_rows = xbar.reshape(-1, feat_size)
    hidden_pre = jnp.dot(node_rows, weight_in, preferred_element_type=jnp.float32) + bias_in
    activation = jax.nn.silu(hidden_pre).astype(jnp.bfloat16)
    logits = jnp.dot(activation, weight_out, preferred_element_type=jnp.float32) + bias_out
    expo = jnp.exp(logits)
    prob = (expo / jnp.sum(expo, -1, keepdims=True)).reshape(row_tiles, samples, tile_size, classes)
    average = jnp.mean(prob, axis=1)
    squares = average * average
    sharp = squares / jnp.sum(squares, -1, keepdims=True)
    onehot = (node_labels.reshape(row_tiles, tile_size)[..., None] == jnp.arange(classes, dtype=jnp.int32)).astype(jnp.float32)
    used = labeled.reshape(row_tiles, 1, tile_size, 1).astype(jnp.float32)
    push = 2.0 * (prob - sharp[:, None])
    inner = jnp.sum(push * prob, -1, keepdims=True)
    dlogits = (used * (prob - onehot[:, None]) + prob * (push - inner)) * scale
    dlogits = dlogits.reshape(-1, classes)
    dlog_b = dlogits.astype(jnp.bfloat16)
    grad_weight_out = jnp.dot(activation.T, dlog_b, preferred_element_type=jnp.float32)
    grad_bias_out = jnp.sum(dlogits, 0)
    dact = jnp.dot(dlog_b, weight_out.T, preferred_element_type=jnp.float32)
    sigma = jax.nn.sigmoid(hidden_pre)
    dpre = dact * sigma * (1.0 + hidden_pre * (1.0 - sigma))
    grad_bias_in = jnp.sum(dpre, 0)
    grad_weight_in = jnp.dot(node_rows.T, dpre.astype(jnp.bfloat16), preferred_element_type=jnp.float32)
    return grad_weight_in, grad_bias_in, grad_weight_out, grad_bias_out


def reference(features, keep_masks, serve_ids, col_slot, adj_blocks, node_labels, labeled, weight_in, bias_in, weight_out, bias_out):
    scale = 1.0 / (SAMPLES * NODE_DEV)

    def one_batch(inputs):
        feats, masks_b, serve_b, slots_b, blocks_b, labels_b, labeled_b = inputs
        columns = column_tiles(serve_b, slots_b)
        own_tiles = feats.reshape(TILES, TILE, FEAT)
        mask_tiles = masks_b.reshape(SAMPLES, TILES, TILE).transpose(1, 0, 2)
        masked = mask_tiles[:, :, :, None] * own_tiles[:, None, :, :]
        total = masked.astype(jnp.float32)
        current = masked
        for step in range(ORDER):
            result = propagate(current, blocks_b, columns)
            total = total + result
            current = result.astype(jnp.bfloat16)
        xbar = (total * (1.0 / ((ORDER + 1) * KEEP_RATE))).astype(jnp.bfloat16)
        return mlp_grads(xbar, labels_b, labeled_b, weight_in, bias_in, weight_out, bias_out, scale)

    stacked = lax.map(one_batch, (features, keep_masks, serve_ids, col_slot, adj_blocks, node_labels, labeled))
    return (jnp.sum(stacked[0], 0), jnp.sum(stacked[1], 0), jnp.sum(stacked[2], 0), jnp.sum(stacked[3], 0))
```

```python
import functools

import jax
import jax.numpy as jnp
from jax import lax
from jax.experimental import pallas as pl
from jax.experimental.pallas import tpu as pltpu
from jax.sharding import PartitionSpec as P

ORDER = 2
KEEP_RATE = 0.5
GROWS = 320
MESH = pl.DeviceIdType.MESH


def place(x, y, z, c):
    return (x * 4 + lax.div(y, 2), z * 4 + lax.rem(y, 2) * 2 + c)


def my_place():
    dp = lax.axis_index("dp")
    dom = lax.axis_index("dom")
    x = lax.div(dp, 4)
    y = lax.rem(dp, 4) * 2 + lax.rem(lax.div(dom, 2), 2)
    z = lax.div(dom, 4)
    c = lax.rem(dom, 2)
    return x, y, z, c


def all_reduce_kernel(
    g_ref, o_ref, core_in, held, first_in, second, second_in, third, third_in, fourth,
    core_s, core_r, one_s, one_r, two_s, two_r, three_s, three_r,
    four_s, four_r, five_s, five_r, six_s, six_r,
):
    x, y, z, c = my_place()
    other = lax.rem(c + 1, 2)
    partner = place(x, y, z, other)
    mine = (z, y)

    def along(axis, d):
        if axis == 0:
            k = lax.rem(z + d, 8)
            return k, place(x, y, k, c)
        k = lax.rem(y + d, 8)
        return k, place(x, k, z, c)

    def remote(src, dst, send_sem, recv_sem, target):
        return pltpu.make_async_remote_copy(
            src_ref=src, dst_ref=dst, send_sem=send_sem, recv_sem=recv_sem,
            device_id=target, device_id_type=MESH,
        )

    def each(start, stop, body):
        def step(i, carry):
            body(i)
            return carry

        lax.fori_loop(start, stop, step, 0)

    barrier = pltpu.get_barrier_semaphore()
    pl.semaphore_signal(barrier, inc=1, device_id=partner, device_id_type=MESH)

    def greet(d):
        for axis in range(2):
            pl.semaphore_signal(barrier, inc=1, device_id=along(axis, d)[1], device_id_type=MESH)

    def greet_x(d):
        target = place(lax.rem(x + d, 4), y, z, c)
        pl.semaphore_signal(barrier, inc=1, device_id=target, device_id_type=MESH)

    each(1, 8, greet)
    each(1, 4, greet_x)
    second[...] = jnp.zeros_like(second)
    pl.semaphore_wait(barrier, 18)

    def core_copy(half, d):
        k = lax.rem(mine[half] + d, 8)
        return remote(
            g_ref.at[other, half, k], core_in.at[half, k],
            core_s.at[half, d], core_r.at[half, d], partner,
        )

    def core_start(i):
        for half in range(2):
            core_copy(half, lax.rem(i, 8)).start()

    each(1, 9, core_start)

    def one_copy(half, d):
        k, target = along(half, d)
        return remote(
            held.at[half, k], first_in.at[half, d - 1],
            one_s.at[half, d - 1], one_r.at[half, d - 1], target,
        )

    def core_add(i):
        d = lax.rem(i, 8)
        for half in range(2):
            k = lax.rem(mine[half] + d, 8)
            core_copy(half, d).wait_recv()
            held[half, k] = g_ref[c, half, k] + core_in[half, k]

    def one_step(d):
        core_add(d)
        for half in range(2):
            one_copy(half, d).start()

    each(1, 8, one_step)
    core_add(8)

    def one_wait(d):
        for half in range(2):
            one_copy(half, d).wait_recv()

    each(1, 8, one_wait)
    for half in range(2):
        total = held[half, mine[half]]
        for d in range(7):
            total = total + first_in[half, d]
        second[half, pl.ds(0, 5)] = total

    def two_copy(half, d):
        k, target = along(1 - half, d)
        return remote(
            second.at[half, k], second_in.at[half, d - 1],
            two_s.at[half, d - 1], two_r.at[half, d - 1], target,
        )

    def two_step(d):
        for half in range(2):
            two_copy(half, d).start()

    def two_wait(d):
        for half in range(2):
            two_copy(half, d).wait_recv()

    each(1, 8, two_step)
    each(1, 8, two_wait)
    for half in range(2):
        total = second[half, mine[1 - half]]
        for d in range(7):
            total = total + second_in[half, d]
        third[half] = total

    def three_copy(d):
        target = place(lax.rem(x + d, 4), y, z, c)
        return remote(third, third_in.at[x], three_s.at[d - 1], three_r.at[d - 1], target)

    each(1, 4, lambda d: three_copy(d).start())
    third_in[x] = third[...]
    each(1, 4, lambda d: three_copy(d).wait_recv())
    total = (third_in[0] + third_in[1]) + (third_in[2] + third_in[3])
    for half in range(2):
        fourth[half, mine[1 - half]] = total[half]

    def four_copy(half, d):
        target = along(1 - half, d)[1]
        piece = fourth.at[half, mine[1 - half]]
        return remote(piece, piece, four_s.at[half, d - 1], four_r.at[half, d - 1], target)

    def four_step(d):
        for half in range(2):
            four_copy(half, d).start()

    def four_wait(d):
        for half in range(2):
            four_copy(half, d).wait_recv()

    each(1, 8, four_step)
    each(1, 8, four_wait)

    def five_copy(half, d):
        target = along(half, d)[1]
        return remote(
            fourth.at[half, pl.ds(0, 5)], o_ref.at[c, half, mine[half]],
            five_s.at[half, d - 1], five_r.at[half, d - 1], target,
        )

    def five_step(d):
        for half in range(2):
            five_copy(half, d).start()

    each(1, 8, five_step)

    def six_copy(half, d):
        k = lax.rem(mine[half] + 8 - d, 8)
        piece = o_ref.at[c, half, k]
        return remote(piece, piece, six_s.at[half, d - 1], six_r.at[half, d - 1], partner)

    def six_own(half):
        return remote(
            fourth.at[half, pl.ds(0, 5)], o_ref.at[c, half, mine[half]],
            six_s.at[half, 7], six_r.at[half, 7], partner,
        )

    for half in range(2):
        six_own(half).start()
        o_ref[c, half, mine[half]] = fourth[half, pl.ds(0, 5)]

    def six_step(d):
        for half in range(2):
            five_copy(half, d).wait_recv()
            six_copy(half, d).start()

    each(1, 8, six_step)

    def finish(d):
        for half in range(2):
            one_copy(half, d).wait_send()
            two_copy(half, d).wait_send()
            four_copy(half, d).wait_send()
            five_copy(half, d).wait_send()
            six_copy(half, d).wait_send()
            six_copy(half, d).wait_recv()

    def finish_core(d):
        for half in range(2):
            core_copy(half, d).wait_send()

    each(1, 8, finish)
    each(0, 8, finish_core)
    each(1, 4, lambda d: three_copy(d).wait_send())
    for half in range(2):
        six_own(half).wait_send()
        six_own(half).wait_recv()


def all_reduce(grads):
    piece = (5, 16, 128)
    f32 = jnp.float32
    dma = pltpu.SemaphoreType.DMA
    shape = (2, 2, 8) + piece
    return pl.pallas_call(
        all_reduce_kernel,
        name="all_reduce",
        out_shape=jax.ShapeDtypeStruct(shape, f32),
        in_specs=[pl.BlockSpec(memory_space=pltpu.VMEM)],
        out_specs=pl.BlockSpec(memory_space=pltpu.VMEM),
        scratch_shapes=[
            pltpu.VMEM((2, 8) + piece, f32),
            pltpu.VMEM((2, 8) + piece, f32),
            pltpu.VMEM((2, 7) + piece, f32),
            pltpu.VMEM((2, 8, 16, 128), f32),
            pltpu.VMEM((2, 7, 16, 128), f32),
            pltpu.VMEM((2, 16, 128), f32),
            pltpu.VMEM((4, 2, 16, 128), f32),
            pltpu.VMEM((2, 8, 16, 128), f32),
        ]
        + [dma((2, 8))] * 2
        + [dma((2, 7))] * 4
        + [dma((3,))] * 2
        + [dma((2, 7))] * 4
        + [dma((2, 8))] * 2,
        compiler_params=pltpu.CompilerParams(collective_id=0, has_side_effects=True),
    )(grads.reshape(shape)).reshape(grads.shape)

def exchange_kernel(chunks, own_ids, ids_ref, src_ref, pool_ref, table_v, table_s, staged, *rest):
    ring, rest = rest[: 7 * chunks], rest[7 * chunks :]
    right_s, right_r, left_s, left_r, side_s, side_r, ids_s, ids_r, table_sem = rest
    x, y, z, c = my_place()
    near = lax.rem(y, 2)
    far_y, far_c = y + 1 - 2 * near, 1 - c
    me = z * 4 + near * 2 + c
    right = place(x, y, lax.rem(z + 1, 8), c)
    left = place(x, y, lax.rem(z + 7, 8), c)
    sides = (
        (place(x, y, z, far_c), z * 4 + near * 2 + far_c),
        (place(x, far_y, z, c), z * 4 + (1 - near) * 2 + c),
        (place(x, far_y, z, far_c), z * 4 + (1 - near) * 2 + far_c),
    )
    half = chunks // 2

    def remote(src, dst, send_sem, recv_sem, target):
        return pltpu.make_async_remote_copy(
            src_ref=src, dst_ref=dst, send_sem=send_sem, recv_sem=recv_sem,
            device_id=target, device_id_type=MESH,
        )

    def held(lane, step, q):
        return ring[6 * chunks + q] if step == 4 else ring[(lane * 3 + step - 1) * chunks + q]

    def along(lane, step, q):
        src = src_ref.at[q] if step == 0 else held(lane, step, q)
        sems = ((right_s, right_r), (left_s, left_r))[lane]
        return remote(
            src, held(lane, step + 1, q), sems[0].at[step, q], sems[1].at[step, q],
            (right, left)[lane],
        )

    def ids_copy(d):
        return remote(
            ids_ref, table_v.at[z], ids_s.at[d - 1], ids_r.at[d - 1],
            place(x, y, lax.rem(z + d, 8), c),
        )

    def carried(lane, step, q):
        return step < 3 or (q < half if lane == 0 else q >= half)

    barrier = pltpu.get_barrier_semaphore()
    for d in range(1, 8):
        pl.semaphore_signal(
            barrier, inc=1, device_id=place(x, y, lax.rem(z + d, 8), c), device_id_type=MESH
        )
    for target, _ in sides:
        pl.semaphore_signal(barrier, inc=1, device_id=target, device_id_type=MESH)
    pl.semaphore_wait(barrier, 10)

    for d in range(1, 8):
        ids_copy(d).start()
    for q in range(chunks):
        for lane in range(2):
            along(lane, 0, q).start()

    def side_copy(i, k, q, source):
        return remote(
            staged.at[i, k, q], pool_ref.at[source * 4 + near * 2 + c, q],
            side_s.at[i, k], side_r.at[i, k], sides[k][0],
        )

    def deliver(i, source, block, q, ids):
        for k in range(3):
            staged[i, k, q] = block(ids(sides[k][1]))
        pool_ref[source * 4 + near * 2 + c, q] = block(ids(me))
        for k in range(3):
            side_copy(i, k, q, source).start()

    for q in range(chunks):
        deliver(0, z, lambda t: src_ref[q, t], q, lambda to: own_ids[to])
    for q in range(chunks):
        for t in range(4):
            pool_ref[32 + t, q] = src_ref[q, t]
    table_v[z] = ids_ref[...]
    for d in range(1, 8):
        ids_copy(d).wait_recv()
    local = pltpu.make_async_copy(table_v, table_s, table_sem)
    local.start()
    local.wait()

    for step in range(1, 4):
        for q in range(chunks):
            for lane in range(2):
                along(lane, step - 1, q).wait_recv()
                if carried(lane, step, q):
                    along(lane, step, q).start()
            for lane in range(2):
                source = lax.rem(z + (8 - step if lane == 0 else step), 8)
                block = held(lane, step, q)
                deliver(
                    1 + lane * 3 + step - 1, source, lambda t: block[t], q,
                    lambda to: table_s[source, 0, to],
                )
    source = lax.rem(z + 4, 8)
    for n in range(half):
        for lane in range(2):
            q = n + lane * half
            along(lane, 3, q).wait_recv()
            block = held(0, 4, q)
            deliver(
                7, source, lambda t: block[t], q, lambda to: table_s[source, 0, to]
            )

    for d in range(1, 8):
        ids_copy(d).wait_send()
    for step in range(4):
        for q in range(chunks):
            for lane in range(2):
                if carried(lane, step, q):
                    along(lane, step, q).wait_send()
    for i in range(8):
        for k in range(3):
            whole = remote(
                staged.at[i, k], pool_ref.at[i], side_s.at[i, k], side_r.at[i, k], sides[k][0]
            )
            whole.wait_send()
            whole.wait_recv()


def exchange(own_ids, ids, tiles, collective_id):
    chunks, count, rows, lanes = tiles.shape
    bf16 = tiles.dtype
    dma = pltpu.SemaphoreType.DMA
    vmem = pl.BlockSpec(memory_space=pltpu.VMEM)
    return pl.pallas_call(
        functools.partial(exchange_kernel, chunks),
        name="exchange",
        out_shape=jax.ShapeDtypeStruct((36, chunks, rows, lanes), bf16),
        in_specs=[pl.BlockSpec(memory_space=pltpu.SMEM), vmem, vmem],
        out_specs=vmem,
        scratch_shapes=[
            pltpu.VMEM((8, 8, 128), jnp.int32),
            pltpu.SMEM((8, 8, 128), jnp.int32),
            pltpu.VMEM((8, 3, chunks, rows, lanes), bf16),
        ]
        + [pltpu.VMEM((count, rows, lanes), bf16)] * (7 * chunks)
        + [dma((4, chunks))] * 4
        + [dma((8, 3))] * 2
        + [dma((7,))] * 2
        + [dma(())],
        compiler_params=pltpu.CompilerParams(collective_id=collective_id, has_side_effects=True),
    )(own_ids, ids, tiles)


def tile_and_masks(pool_ref, slot):
    half = 64
    tile = jnp.concatenate([pool_ref[slot, 0, :half], pool_ref[slot, 1, :half]], 0)
    masks = [pool_ref[slot, q, half + i : half + i + 1] for q in range(2) for i in range(2)]
    return tile, masks


def hop_one_kernel(slots_ref, adj_ref, pool_ref, current_ref, base_ref):
    f32 = jnp.float32
    rows = lax.broadcasted_iota(jnp.int32, (128, 128), 0)
    cols = lax.broadcasted_iota(jnp.int32, (128, 128), 1)
    eye = jnp.where(rows == cols, 1.0, 0.0).astype(jnp.bfloat16)

    def row_tile(r, carry):
        own, own_masks = tile_and_masks(pool_ref, 32 + r)
        own_block = jnp.concatenate([eye * m for m in own_masks], 0)
        masked = jnp.dot(own_block, own, preferred_element_type=f32)
        result = jnp.zeros((512, 128), f32)
        for j in range(0, 10, 2):
            blocks, tiles = [], []
            for i in range(2):
                tile, masks = tile_and_masks(pool_ref, slots_ref[r, j + i])
                block = adj_ref[r, j + i]
                blocks.append(jnp.concatenate([block * m for m in masks], 0))
                tiles.append(tile)
            result += jnp.dot(
                jnp.concatenate(blocks, 1), jnp.concatenate(tiles, 0), preferred_element_type=f32
            )
        for s in range(4):
            part = result[s * 128 : (s + 1) * 128]
            current_ref[s, r] = part.astype(jnp.bfloat16)
            base_ref[r, s] = masked[s * 128 : (s + 1) * 128] + part
        return carry

    lax.fori_loop(0, 4, row_tile, 0)


def hop_one(slots, adj, pool):
    vmem = pl.BlockSpec(memory_space=pltpu.VMEM)
    return pl.pallas_call(
        hop_one_kernel,
        name="hop_one",
        out_shape=(
            jax.ShapeDtypeStruct((4, 4, 128, 128), jnp.bfloat16),
            jax.ShapeDtypeStruct((4, 4, 128, 128), jnp.float32),
        ),
        in_specs=[pl.BlockSpec(memory_space=pltpu.SMEM), vmem, vmem],
        out_specs=(vmem, vmem),
    )(slots, adj, pool)


def column(row):
    return jnp.broadcast_to(row, (128, 128)).T[:, :1]


def mlp_kernel(
    slots_ref, adj_ref, pool_ref, base_ref, labels_ref, labeled_ref,
    w_in_ref, b_in_ref, w_out_ref, b_out_ref, g_ref,
    xbar, xbar_t, act, slope, dlog, dlog_t,
):
    f32, bf16 = jnp.float32, jnp.bfloat16
    classes = w_out_ref.shape[0]
    nt = (((1,), (1,)), ((), ()))
    g_ref[...] = jnp.zeros_like(g_ref)

    def row_tile(r, bias_total):
        hop = jnp.zeros((128, 512), f32)
        for j in range(0, 10, 2):
            lhs = jnp.concatenate([adj_ref[r, j], adj_ref[r, j + 1]], 1)
            rhs = jnp.concatenate(
                [
                    jnp.concatenate([pool_ref[slots_ref[r, j + i], s] for s in range(4)], 1)
                    for i in range(2)
                ],
                0,
            )
            hop += jnp.dot(lhs, rhs, preferred_element_type=f32)
        for s in range(4):
            mean = (base_ref[r, s] + hop[:, s * 128 : (s + 1) * 128]) * (
                1.0 / ((ORDER + 1) * KEEP_RATE)
            )
            xbar[r, s * 128 : (s + 1) * 128] = mean.astype(bf16)
            xbar_t[r, :, s * 128 : (s + 1) * 128] = mean.T.astype(bf16)

        rows = xbar[r]
        logits = jnp.zeros((512, classes), f32) + b_out_ref[...]
        for h in range(4):
            cols = slice(h * 256, (h + 1) * 256)
            pre = jnp.dot(rows, w_in_ref[:, cols], preferred_element_type=f32) + b_in_ref[:, cols]
            sigma = 1.0 / (1.0 + jnp.exp(-pre))
            hidden = (pre * sigma).astype(bf16)
            act[h, r] = hidden
            slope[h, r] = sigma * (1.0 + pre * (1.0 - sigma))
            logits += lax.dot_general(hidden, w_out_ref[:, cols], nt, preferred_element_type=f32)

        expo = jnp.exp(logits)
        prob = expo / jnp.sum(expo, -1, keepdims=True)
        parts = [prob[s * 128 : (s + 1) * 128] for s in range(4)]
        average = (parts[0] + parts[1] + parts[2] + parts[3]) * 0.25
        squares = average * average
        sharp = squares / jnp.sum(squares, -1, keepdims=True)
        label = column(labels_ref[pl.ds(r, 1), :].astype(f32)).astype(jnp.int32)
        used = column(labeled_ref[pl.ds(r, 1), :].astype(f32))
        onehot = (label == lax.broadcasted_iota(jnp.int32, (128, classes), 1)).astype(f32)
        for s in range(4):
            push = 2.0 * (parts[s] - sharp)
            inner = jnp.sum(push * parts[s], -1, keepdims=True)
            dlogits = (used * (parts[s] - onehot) + parts[s] * (push - inner)) * (1.0 / 2048.0)
            bias_total = bias_total + jnp.sum(dlogits, 0, keepdims=True)
            dlog[r, s * 128 : (s + 1) * 128] = dlogits.astype(bf16)
            dlog_t[r, :, s * 128 : (s + 1) * 128] = dlogits.T.astype(bf16)
        return bias_total

    bias_total = lax.fori_loop(0, 4, row_tile, jnp.zeros((1, classes), f32))
    g_ref[0, 301:302, :] = bias_total[:, :128]
    g_ref[1, 301:302, : classes - 128] = bias_total[:, 128:]

    for h in range(4):
        cols = slice(h * 256, (h + 1) * 256)

        def back(r, carry):
            w_in_grad, w_out_grad, b_in_grad = carry
            dact = jnp.dot(dlog[r], w_out_ref[:, cols], preferred_element_type=f32)
            dpre = dact * slope[h, r]
            w_in_grad = w_in_grad + jnp.dot(
                xbar_t[r], dpre.astype(bf16), preferred_element_type=f32
            )
            w_out_grad = w_out_grad + jnp.dot(dlog_t[r], act[h, r], preferred_element_type=f32)
            b_in_grad = b_in_grad + jnp.sum(dpre, 0, keepdims=True)
            return w_in_grad, w_out_grad, b_in_grad

        w_in_grad, w_out_grad, b_in_grad = lax.fori_loop(
            0, 4, back,
            (jnp.zeros((128, 256), f32), jnp.zeros((classes, 256), f32), jnp.zeros((1, 256), f32)),
        )
        for i in range(2):
            lanes = slice(i * 128, (i + 1) * 128)
            g_ref[2 * h + i, :128] = w_in_grad[:, lanes]
            g_ref[2 * h + i, 128 : 128 + classes] = w_out_grad[:, lanes]
            g_ref[2 * h + i, 300:301] = b_in_grad[:, lanes]


def mlp(slots, adj, pool, base, labels, labeled, w_in, b_in, w_out_t, b_out):
    vmem = pl.BlockSpec(memory_space=pltpu.VMEM)
    classes = w_out_t.shape[0]
    bf16 = jnp.bfloat16
    return pl.pallas_call(
        mlp_kernel,
        name="mlp",
        out_shape=jax.ShapeDtypeStruct((8, GROWS, 128), jnp.float32),
        in_specs=[pl.BlockSpec(memory_space=pltpu.SMEM)] + [vmem] * 9,
        out_specs=vmem,
        scratch_shapes=[
            pltpu.VMEM((4, 512, 128), bf16),
            pltpu.VMEM((4, 128, 512), bf16),
            pltpu.VMEM((4, 4, 512, 256), bf16),
            pltpu.VMEM((4, 4, 512, 256), jnp.float32),
            pltpu.VMEM((4, 512, classes), bf16),
            pltpu.VMEM((4, classes, 512), bf16),
        ],
    )(slots, adj, pool, base, labels, labeled, w_in, b_in, w_out_t, b_out)


def unpack_kernel(g_ref, w_in_ref, b_in_ref, w_out_ref, b_out_ref):
    classes = w_out_ref.shape[0]
    for i in range(8):
        lanes = slice(i * 128, (i + 1) * 128)
        w_in_ref[:, lanes] = g_ref[i, :128]
        w_out_ref[:, lanes] = g_ref[i, 128 : 128 + classes]
        b_in_ref[:, lanes] = g_ref[i, 300:301]
    b_out_ref[:, :128] = g_ref[0, 301:302]
    b_out_ref[:, 128:] = g_ref[1, 301:302, : classes - 128]


def unpack(summed, classes):
    vmem = pl.BlockSpec(memory_space=pltpu.VMEM)
    shapes = ((128, 1024), (1, 1024), (classes, 1024), (1, classes))
    return pl.pallas_call(
        unpack_kernel,
        name="unpack",
        out_shape=tuple(jax.ShapeDtypeStruct(s, jnp.float32) for s in shapes),
        in_specs=[vmem],
        out_specs=(vmem,) * 4,
    )(summed)


def per_device(
    features, keep_masks, serve_ids, col_slot, adj_blocks, node_labels, labeled,
    weight_in, bias_in, weight_out, bias_out,
):
    classes = weight_out.shape[1]
    own_ids = serve_ids.reshape(-1)
    ids = jnp.pad(own_ids[None], ((0, 7), (0, 96)))
    slots, adj = col_slot[0], adj_blocks[0]
    tiles = features.reshape(4, 2, 64, 128).transpose(1, 0, 2, 3)
    masks = keep_masks.reshape(2, 2, 4, 128).transpose(0, 2, 1, 3)
    both = jnp.concatenate([tiles, jnp.pad(masks, ((0, 0), (0, 0), (0, 6), (0, 0)))], 2)
    pool = exchange(own_ids, ids, both, 1)
    current, base = hop_one(slots, adj, pool)
    pool = exchange(own_ids, ids, current, 2)
    grads = mlp(
        slots, adj, pool, base, node_labels.reshape(4, 128), labeled.reshape(4, 128),
        weight_in, bias_in[None], weight_out.T, bias_out[None],
    )
    w_in, b_in, w_out_t, b_out = unpack(all_reduce(grads), classes)
    return (w_in, b_in[0], w_out_t.T, b_out[0])


def solution(mesh):
    placed = (
        P("dp", "dom", None),
        P("dp", None, "dom"),
        P("dp", "dom", None, None),
        P("dp", "dom", None),
        P("dp", "dom", None, None, None),
        P("dp", "dom"),
        P("dp", "dom"),
        P(),
        P(),
        P(),
        P(),
    )
    return jax.shard_map(
        per_device, mesh=mesh, in_specs=placed, out_specs=(P(), P(), P(), P()), check_vma=False
    )
```

```python
import jax
import jax.numpy as jnp
from jax import lax
from jax.experimental import pallas as pl
from jax.experimental.pallas import tpu as pltpu
from jax.sharding import PartitionSpec as P

ORDER = 2
KEEP_RATE = 0.5
GROWS = 320
MESH = pl.DeviceIdType.MESH


def place(x, y, z, c):
    return (x * 4 + lax.div(y, 2), z * 4 + lax.rem(y, 2) * 2 + c)


def my_place():
    dp = lax.axis_index("dp")
    dom = lax.axis_index("dom")
    x = lax.div(dp, 4)
    y = lax.rem(dp, 4) * 2 + lax.rem(lax.div(dom, 2), 2)
    z = lax.div(dom, 4)
    c = lax.rem(dom, 2)
    return x, y, z, c


def all_reduce_kernel(
    g_ref, o_ref, core_in, held, first_in, second, second_in, third, third_in, fourth,
    core_s, core_r, one_s, one_r, two_s, two_r, three_s, three_r,
    four_s, four_r, five_s, five_r, six_s, six_r,
):
    x, y, z, c = my_place()
    other = lax.rem(c + 1, 2)
    partner = place(x, y, z, other)
    mine = (z, y)

    def along(axis, d):
        if axis == 0:
            k = lax.rem(z + d, 8)
            return k, place(x, y, k, c)
        k = lax.rem(y + d, 8)
        return k, place(x, k, z, c)

    def remote(src, dst, send_sem, recv_sem, target):
        return pltpu.make_async_remote_copy(
            src_ref=src, dst_ref=dst, send_sem=send_sem, recv_sem=recv_sem,
            device_id=target, device_id_type=MESH,
        )

    def each(start, stop, body):
        def step(i, carry):
            body(i)
            return carry

        lax.fori_loop(start, stop, step, 0)

    barrier = pltpu.get_barrier_semaphore()
    pl.semaphore_signal(barrier, inc=1, device_id=partner, device_id_type=MESH)

    def greet(d):
        for axis in range(2):
            pl.semaphore_signal(barrier, inc=1, device_id=along(axis, d)[1], device_id_type=MESH)

    def greet_x(d):
        target = place(lax.rem(x + d, 4), y, z, c)
        pl.semaphore_signal(barrier, inc=1, device_id=target, device_id_type=MESH)

    each(1, 8, greet)
    each(1, 4, greet_x)
    second[...] = jnp.zeros_like(second)
    pl.semaphore_wait(barrier, 18)

    def core_copy(half, d):
        k = lax.rem(mine[half] + d, 8)
        return remote(
            g_ref.at[other, half, k], core_in.at[half, k],
            core_s.at[half, d], core_r.at[half, d], partner,
        )

    def core_start(i):
        for half in range(2):
            core_copy(half, lax.rem(i, 8)).start()

    each(1, 9, core_start)

    def one_copy(half, d):
        k, target = along(half, d)
        return remote(
            held.at[half, k], first_in.at[half, d - 1],
            one_s.at[half, d - 1], one_r.at[half, d - 1], target,
        )

    def core_add(i):
        d = lax.rem(i, 8)
        for half in range(2):
            k = lax.rem(mine[half] + d, 8)
            core_copy(half, d).wait_recv()
            held[half, k] = g_ref[c, half, k] + core_in[half, k]

    def one_step(d):
        core_add(d)
        for half in range(2):
            one_copy(half, d).start()

    each(1, 8, one_step)
    core_add(8)

    def one_wait(d):
        for half in range(2):
            one_copy(half, d).wait_recv()

    each(1, 8, one_wait)
    for half in range(2):
        total = held[half, mine[half]]
        for d in range(7):
            total = total + first_in[half, d]
        second[half, pl.ds(0, 5)] = total

    def two_copy(half, d):
        k, target = along(1 - half, d)
        return remote(
            second.at[half, k], second_in.at[half, d - 1],
            two_s.at[half, d - 1], two_r.at[half, d - 1], target,
        )

    def two_step(d):
        for half in range(2):
            two_copy(half, d).start()

    def two_wait(d):
        for half in range(2):
            two_copy(half, d).wait_recv()

    each(1, 8, two_step)
    each(1, 8, two_wait)
    for half in range(2):
        total = second[half, mine[1 - half]]
        for d in range(7):
            total = total + second_in[half, d]
        third[half] = total

    def three_copy(d):
        target = place(lax.rem(x + d, 4), y, z, c)
        return remote(third, third_in.at[x], three_s.at[d - 1], three_r.at[d - 1], target)

    each(1, 4, lambda d: three_copy(d).start())
    third_in[x] = third[...]
    each(1, 4, lambda d: three_copy(d).wait_recv())
    total = (third_in[0] + third_in[1]) + (third_in[2] + third_in[3])
    for half in range(2):
        fourth[half, mine[1 - half]] = total[half]

    def four_copy(half, d):
        target = along(1 - half, d)[1]
        piece = fourth.at[half, mine[1 - half]]
        return remote(piece, piece, four_s.at[half, d - 1], four_r.at[half, d - 1], target)

    def four_step(d):
        for half in range(2):
            four_copy(half, d).start()

    def four_wait(d):
        for half in range(2):
            four_copy(half, d).wait_recv()

    each(1, 8, four_step)
    each(1, 8, four_wait)

    def five_copy(half, d):
        target = along(half, d)[1]
        return remote(
            fourth.at[half, pl.ds(0, 5)], o_ref.at[c, half, mine[half]],
            five_s.at[half, d - 1], five_r.at[half, d - 1], target,
        )

    def five_step(d):
        for half in range(2):
            five_copy(half, d).start()

    each(1, 8, five_step)

    def six_copy(half, d):
        k = lax.rem(mine[half] + 8 - d, 8)
        piece = o_ref.at[c, half, k]
        return remote(piece, piece, six_s.at[half, d - 1], six_r.at[half, d - 1], partner)

    def six_own(half):
        return remote(
            fourth.at[half, pl.ds(0, 5)], o_ref.at[c, half, mine[half]],
            six_s.at[half, 7], six_r.at[half, 7], partner,
        )

    for half in range(2):
        six_own(half).start()
        o_ref[c, half, mine[half]] = fourth[half, pl.ds(0, 5)]

    def six_step(d):
        for half in range(2):
            five_copy(half, d).wait_recv()
            six_copy(half, d).start()

    each(1, 8, six_step)

    def finish(d):
        for half in range(2):
            one_copy(half, d).wait_send()
            two_copy(half, d).wait_send()
            four_copy(half, d).wait_send()
            five_copy(half, d).wait_send()
            six_copy(half, d).wait_send()
            six_copy(half, d).wait_recv()

    def finish_core(d):
        for half in range(2):
            core_copy(half, d).wait_send()

    each(1, 8, finish)
    each(0, 8, finish_core)
    each(1, 4, lambda d: three_copy(d).wait_send())
    for half in range(2):
        six_own(half).wait_send()
        six_own(half).wait_recv()


def all_reduce(grads):
    piece = (5, 16, 128)
    f32 = jnp.float32
    dma = pltpu.SemaphoreType.DMA
    shape = (2, 2, 8) + piece
    return pl.pallas_call(
        all_reduce_kernel,
        name="all_reduce",
        out_shape=jax.ShapeDtypeStruct(shape, f32),
        in_specs=[pl.BlockSpec(memory_space=pltpu.VMEM)],
        out_specs=pl.BlockSpec(memory_space=pltpu.VMEM),
        scratch_shapes=[
            pltpu.VMEM((2, 8) + piece, f32),
            pltpu.VMEM((2, 8) + piece, f32),
            pltpu.VMEM((2, 7) + piece, f32),
            pltpu.VMEM((2, 8, 16, 128), f32),
            pltpu.VMEM((2, 7, 16, 128), f32),
            pltpu.VMEM((2, 16, 128), f32),
            pltpu.VMEM((4, 2, 16, 128), f32),
            pltpu.VMEM((2, 8, 16, 128), f32),
        ]
        + [dma((2, 8))] * 2
        + [dma((2, 7))] * 4
        + [dma((3,))] * 2
        + [dma((2, 7))] * 4
        + [dma((2, 8))] * 2,
        compiler_params=pltpu.CompilerParams(collective_id=0, has_side_effects=True),
    )(grads.reshape(shape)).reshape(grads.shape)

def spread_kernel(
    own_ids, slots_ref, ids_ref, feat_ref, mask_ref, adj_ref, pool_ref, base_ref,
    ids_v, table_v, table_s, src, first_pool, current, staged_one, staged_two, *rest,
):
    f32, bf16 = jnp.float32, jnp.bfloat16
    rings = (rest[:14], rest[14:42])
    sems = (rest[42:48], rest[48:54])
    ids_s, ids_r, table_sem = rest[54:]
    x, y, z, c = my_place()
    near = lax.rem(y, 2)
    far_y, far_c = y + 1 - 2 * near, 1 - c
    me = z * 4 + near * 2 + c
    turn = (place(x, y, lax.rem(z + 1, 8), c), place(x, y, lax.rem(z + 7, 8), c))
    sides = (
        (place(x, far_y, z, c), z * 4 + (1 - near) * 2 + c),
        (place(x, far_y, z, far_c), z * 4 + (1 - near) * 2 + far_c),
        (place(x, y, z, far_c), z * 4 + near * 2 + far_c),
    )

    def remote(from_ref, to_ref, send_sem, recv_sem, target):
        return pltpu.make_async_remote_copy(
            src_ref=from_ref, dst_ref=to_ref, send_sem=send_sem, recv_sem=recv_sem,
            device_id=target, device_id_type=MESH,
        )

    barrier = pltpu.get_barrier_semaphore()
    for d in range(1, 8):
        pl.semaphore_signal(
            barrier, inc=1, device_id=place(x, y, lax.rem(z + d, 8), c), device_id_type=MESH
        )
    for target, _ in sides:
        pl.semaphore_signal(barrier, inc=1, device_id=target, device_id_type=MESH)

    ids_v[...] = jnp.zeros_like(ids_v)
    ids_v[0:1, 0:32] = ids_ref[...]
    masks = mask_ref[...].astype(f32)
    for q in range(2):
        for t in range(4):
            begin = t * 128 + q * 64
            src[q, t, 0:64] = feat_ref[begin : begin + 64]
            pair = masks[2 * q : 2 * q + 2, t * 128 : (t + 1) * 128]
            src[q, t, 64:72] = jnp.concatenate([pair, jnp.zeros((6, 128), f32)], 0).astype(bf16)
            first_pool[32 + t, q] = src[q, t]
    pl.semaphore_wait(barrier, 10)

    def ids_copy(d):
        return remote(
            ids_v, table_v.at[z], ids_s.at[d - 1], ids_r.at[d - 1],
            place(x, y, lax.rem(z + d, 8), c),
        )

    def learn_ids():
        table_v[z] = ids_v[...]
        for d in range(1, 8):
            ids_copy(d).wait_recv()
        local = pltpu.make_async_copy(table_v, table_s, table_sem)
        local.start()
        local.wait()

    def swap(chunks, src_ref, out, staged, ring, marks, ready, before_others):
        lane_s, lane_r = marks[0:2], marks[2:4]
        side_s, side_r = marks[4:6]
        half = chunks // 2

        def held(lane, step, q):
            return ring[6 * chunks + q] if step == 4 else ring[(lane * 3 + step - 1) * chunks + q]

        def along(lane, step, q):
            block = src_ref.at[q] if step == 0 else held(lane, step, q)
            return remote(
                block, held(lane, step + 1, q), lane_s[lane].at[step, q],
                lane_r[lane].at[step, q], turn[lane],
            )

        def carried(lane, step, q):
            return step < 3 or (q < half if lane == 0 else q >= half)

        def side_copy(i, k, q, source):
            return remote(
                staged.at[i, k, q], out.at[source * 4 + near * 2 + c, q],
                side_s.at[i, k], side_r.at[i, k], sides[k][0],
            )

        def deliver(i, source, block, q, ids):
            for k in range(3):
                staged[i, k, q] = block(ids(sides[k][1]))
            out[source * 4 + near * 2 + c, q] = block(ids(me))
            for k in range(3):
                side_copy(i, k, q, source).start()

        for q in range(chunks):
            ready(q)
            for lane in range(2):
                along(lane, 0, q).start()
            deliver(0, z, lambda t: src_ref[q, t], q, lambda to: own_ids[to])
        before_others()
        for step in range(1, 4):
            for q in range(chunks):
                for lane in range(2):
                    along(lane, step - 1, q).wait_recv()
                    if carried(lane, step, q):
                        along(lane, step, q).start()
                for lane in range(2):
                    source = lax.rem(z + (8 - step if lane == 0 else step), 8)
                    block = held(lane, step, q)
                    deliver(
                        1 + lane * 3 + step - 1, source, lambda t: block[t], q,
                        lambda to: table_s[source, 0, to],
                    )
        source = lax.rem(z + 4, 8)
        for n in range(half):
            for lane in range(2):
                q = n + lane * half
                along(lane, 3, q).wait_recv()
                block = held(0, 4, q)
                deliver(7, source, lambda t: block[t], q, lambda to: table_s[source, 0, to])
        for i in range(8):
            for k in range(3):
                remote(
                    staged.at[i, k], out.at[i], side_s.at[i, k], side_r.at[i, k], sides[k][0]
                ).wait_recv()

        def finish():
            for step in range(4):
                for q in range(chunks):
                    for lane in range(2):
                        if carried(lane, step, q):
                            along(lane, step, q).wait_send()
            for i in range(8):
                for k in range(3):
                    remote(
                        staged.at[i, k], out.at[i], side_s.at[i, k], side_r.at[i, k], sides[k][0]
                    ).wait_send()

        return finish

    for d in range(1, 8):
        ids_copy(d).start()
    finish_one = swap(
        2, src, first_pool, staged_one, rings[0], sems[0], lambda q: None, learn_ids
    )

    eye = jnp.where(
        lax.broadcasted_iota(jnp.int32, (128, 128), 0)
        == lax.broadcasted_iota(jnp.int32, (128, 128), 1),
        1.0, 0.0,
    ).astype(bf16)

    def first_hop(s):
        def tile_and_mask(slot):
            tile = jnp.concatenate([first_pool[slot, 0, 0:64], first_pool[slot, 1, 0:64]], 0)
            row = 64 + s % 2
            return tile, first_pool[slot, s // 2, row : row + 1]

        def row_tile(r, carry):
            own, mask = tile_and_mask(32 + r)
            masked = jnp.dot(eye * mask, own, preferred_element_type=f32)
            result = jnp.zeros((128, 128), f32)
            for j in range(0, 10, 2):
                blocks, tiles = [], []
                for i in range(2):
                    tile, mask = tile_and_mask(slots_ref[r, j + i])
                    blocks.append(adj_ref[r, j + i] * mask)
                    tiles.append(tile)
                result += jnp.dot(
                    jnp.concatenate(blocks, 1), jnp.concatenate(tiles, 0),
                    preferred_element_type=f32,
                )
            current[s, r] = result.astype(bf16)
            base_ref[r, s] = masked + result
            return carry

        lax.fori_loop(0, 4, row_tile, 0)

    def own_tiles():
        for q in range(4):
            for t in range(4):
                pool_ref[32 + t, q] = current[q, t]

    finish_two = swap(
        4, current, pool_ref, staged_two, rings[1], sems[1], first_hop, own_tiles
    )
    for d in range(1, 8):
        ids_copy(d).wait_send()
    finish_one()
    finish_two()


def spread(own_ids, slots, features, masks, adj):
    bf16, f32, i32 = jnp.bfloat16, jnp.float32, jnp.int32
    dma = pltpu.SemaphoreType.DMA
    vmem = pl.BlockSpec(memory_space=pltpu.VMEM)
    smem = pl.BlockSpec(memory_space=pltpu.SMEM)

    def marks(chunks):
        return [dma((4, chunks))] * 4 + [dma((8, 3))] * 2

    return pl.pallas_call(
        spread_kernel,
        name="spread",
        out_shape=(
            jax.ShapeDtypeStruct((36, 4, 128, 128), bf16),
            jax.ShapeDtypeStruct((4, 4, 128, 128), f32),
        ),
        in_specs=[smem, smem] + [vmem] * 4,
        out_specs=(vmem, vmem),
        scratch_shapes=[
            pltpu.VMEM((8, 128), i32),
            pltpu.VMEM((8, 8, 128), i32),
            pltpu.SMEM((8, 8, 128), i32),
            pltpu.VMEM((2, 4, 72, 128), bf16),
            pltpu.VMEM((36, 2, 72, 128), bf16),
            pltpu.VMEM((4, 4, 128, 128), bf16),
            pltpu.VMEM((8, 3, 2, 72, 128), bf16),
            pltpu.VMEM((8, 3, 4, 128, 128), bf16),
        ]
        + [pltpu.VMEM((4, 72, 128), bf16)] * 14
        + [pltpu.VMEM((4, 128, 128), bf16)] * 28
        + marks(2)
        + marks(4)
        + [dma((7,)), dma((7,)), dma(())],
        compiler_params=pltpu.CompilerParams(collective_id=1, has_side_effects=True),
    )(own_ids, slots, own_ids[None], features, masks, adj)


def column(row):
    return jnp.broadcast_to(row, (128, 128)).T[:, :1]


def mlp_kernel(
    slots_ref, adj_ref, pool_ref, base_ref, labels_ref, labeled_ref,
    w_in_ref, b_in_ref, w_out_ref, b_out_ref, g_ref,
    xbar, xbar_t, act, slope, dlog, dlog_t,
):
    f32, bf16 = jnp.float32, jnp.bfloat16
    classes = w_out_ref.shape[0]
    nt = (((1,), (1,)), ((), ()))
    g_ref[...] = jnp.zeros_like(g_ref)

    def row_tile(r, bias_total):
        hop = jnp.zeros((128, 512), f32)
        for j in range(0, 10, 2):
            lhs = jnp.concatenate([adj_ref[r, j], adj_ref[r, j + 1]], 1)
            rhs = jnp.concatenate(
                [
                    jnp.concatenate([pool_ref[slots_ref[r, j + i], s] for s in range(4)], 1)
                    for i in range(2)
                ],
                0,
            )
            hop += jnp.dot(lhs, rhs, preferred_element_type=f32)
        for s in range(4):
            mean = (base_ref[r, s] + hop[:, s * 128 : (s + 1) * 128]) * (
                1.0 / ((ORDER + 1) * KEEP_RATE)
            )
            xbar[r, s * 128 : (s + 1) * 128] = mean.astype(bf16)
            xbar_t[r, :, s * 128 : (s + 1) * 128] = mean.T.astype(bf16)

        rows = xbar[r]
        logits = jnp.zeros((512, classes), f32) + b_out_ref[...]
        for h in range(4):
            cols = slice(h * 256, (h + 1) * 256)
            pre = jnp.dot(rows, w_in_ref[:, cols], preferred_element_type=f32) + b_in_ref[:, cols]
            sigma = 1.0 / (1.0 + jnp.exp(-pre))
            hidden = (pre * sigma).astype(bf16)
            act[h, r] = hidden
            slope[h, r] = sigma * (1.0 + pre * (1.0 - sigma))
            logits += lax.dot_general(hidden, w_out_ref[:, cols], nt, preferred_element_type=f32)

        expo = jnp.exp(logits)
        prob = expo / jnp.sum(expo, -1, keepdims=True)
        parts = [prob[s * 128 : (s + 1) * 128] for s in range(4)]
        average = (parts[0] + parts[1] + parts[2] + parts[3]) * 0.25
        squares = average * average
        sharp = squares / jnp.sum(squares, -1, keepdims=True)
        label = column(labels_ref[pl.ds(r, 1), :].astype(f32)).astype(jnp.int32)
        used = column(labeled_ref[pl.ds(r, 1), :].astype(f32))
        onehot = (label == lax.broadcasted_iota(jnp.int32, (128, classes), 1)).astype(f32)
        for s in range(4):
            push = 2.0 * (parts[s] - sharp)
            inner = jnp.sum(push * parts[s], -1, keepdims=True)
            dlogits = (used * (parts[s] - onehot) + parts[s] * (push - inner)) * (1.0 / 2048.0)
            bias_total = bias_total + jnp.sum(dlogits, 0, keepdims=True)
            dlog[r, s * 128 : (s + 1) * 128] = dlogits.astype(bf16)
            dlog_t[r, :, s * 128 : (s + 1) * 128] = dlogits.T.astype(bf16)
        return bias_total

    bias_total = lax.fori_loop(0, 4, row_tile, jnp.zeros((1, classes), f32))
    g_ref[0, 301:302, :] = bias_total[:, :128]
    g_ref[1, 301:302, : classes - 128] = bias_total[:, 128:]

    for h in range(4):
        cols = slice(h * 256, (h + 1) * 256)

        def back(r, carry):
            w_in_grad, w_out_grad, b_in_grad = carry
            dact = jnp.dot(dlog[r], w_out_ref[:, cols], preferred_element_type=f32)
            dpre = dact * slope[h, r]
            w_in_grad = w_in_grad + jnp.dot(
                xbar_t[r], dpre.astype(bf16), preferred_element_type=f32
            )
            w_out_grad = w_out_grad + jnp.dot(dlog_t[r], act[h, r], preferred_element_type=f32)
            b_in_grad = b_in_grad + jnp.sum(dpre, 0, keepdims=True)
            return w_in_grad, w_out_grad, b_in_grad

        w_in_grad, w_out_grad, b_in_grad = lax.fori_loop(
            0, 4, back,
            (jnp.zeros((128, 256), f32), jnp.zeros((classes, 256), f32), jnp.zeros((1, 256), f32)),
        )
        for i in range(2):
            lanes = slice(i * 128, (i + 1) * 128)
            g_ref[2 * h + i, :128] = w_in_grad[:, lanes]
            g_ref[2 * h + i, 128 : 128 + classes] = w_out_grad[:, lanes]
            g_ref[2 * h + i, 300:301] = b_in_grad[:, lanes]


def mlp(slots, adj, pool, base, labels, labeled, w_in, b_in, w_out_t, b_out):
    vmem = pl.BlockSpec(memory_space=pltpu.VMEM)
    classes = w_out_t.shape[0]
    bf16 = jnp.bfloat16
    return pl.pallas_call(
        mlp_kernel,
        name="mlp",
        out_shape=jax.ShapeDtypeStruct((8, GROWS, 128), jnp.float32),
        in_specs=[pl.BlockSpec(memory_space=pltpu.SMEM)] + [vmem] * 9,
        out_specs=vmem,
        scratch_shapes=[
            pltpu.VMEM((4, 512, 128), bf16),
            pltpu.VMEM((4, 128, 512), bf16),
            pltpu.VMEM((4, 4, 512, 256), bf16),
            pltpu.VMEM((4, 4, 512, 256), jnp.float32),
            pltpu.VMEM((4, 512, classes), bf16),
            pltpu.VMEM((4, classes, 512), bf16),
        ],
    )(slots, adj, pool, base, labels, labeled, w_in, b_in, w_out_t, b_out)


def unpack_kernel(g_ref, w_in_ref, b_in_ref, w_out_ref, b_out_ref):
    classes = w_out_ref.shape[0]
    for i in range(8):
        lanes = slice(i * 128, (i + 1) * 128)
        w_in_ref[:, lanes] = g_ref[i, :128]
        w_out_ref[:, lanes] = g_ref[i, 128 : 128 + classes]
        b_in_ref[:, lanes] = g_ref[i, 300:301]
    b_out_ref[:, :128] = g_ref[0, 301:302]
    b_out_ref[:, 128:] = g_ref[1, 301:302, : classes - 128]


def unpack(summed, classes):
    vmem = pl.BlockSpec(memory_space=pltpu.VMEM)
    shapes = ((128, 1024), (1, 1024), (classes, 1024), (1, classes))
    return pl.pallas_call(
        unpack_kernel,
        name="unpack",
        out_shape=tuple(jax.ShapeDtypeStruct(s, jnp.float32) for s in shapes),
        in_specs=[vmem],
        out_specs=(vmem,) * 4,
    )(summed)


def per_device(
    features, keep_masks, serve_ids, col_slot, adj_blocks, node_labels, labeled,
    weight_in, bias_in, weight_out, bias_out,
):
    classes = weight_out.shape[1]
    slots, adj = col_slot[0], adj_blocks[0]
    pool, base = spread(serve_ids.reshape(-1), slots, features[0], keep_masks[0], adj)
    grads = mlp(
        slots, adj, pool, base, node_labels.reshape(4, 128), labeled.reshape(4, 128),
        weight_in, bias_in[None], weight_out.T, bias_out[None],
    )
    w_in, b_in, w_out_t, b_out = unpack(all_reduce(grads), classes)
    return (w_in, b_in[0], w_out_t.T, b_out[0])


def solution(mesh):
    placed = (
        P("dp", "dom", None),
        P("dp", None, "dom"),
        P("dp", "dom", None, None),
        P("dp", "dom", None),
        P("dp", "dom", None, None, None),
        P("dp", "dom"),
        P("dp", "dom"),
        P(),
        P(),
        P(),
        P(),
    )
    return jax.shard_map(
        per_device, mesh=mesh, in_specs=placed, out_specs=(P(), P(), P(), P()), check_vma=False
    )
```

```python
import jax
import jax.numpy as jnp
from jax import lax
from jax.experimental import pallas as pl
from jax.experimental.pallas import tpu as pltpu
from jax.sharding import PartitionSpec as P

ORDER = 2
KEEP_RATE = 0.5
GROWS = 320
MESH = pl.DeviceIdType.MESH


def place(x, y, z, c):
    return (x * 4 + lax.div(y, 2), z * 4 + lax.rem(y, 2) * 2 + c)


def my_place():
    dp = lax.axis_index("dp")
    dom = lax.axis_index("dom")
    x = lax.div(dp, 4)
    y = lax.rem(dp, 4) * 2 + lax.rem(lax.div(dom, 2), 2)
    z = lax.div(dom, 4)
    c = lax.rem(dom, 2)
    return x, y, z, c

def spread_kernel(
    own_ids, slots_ref, ids_ref, feat_ref, mask_ref, adj_ref, pool_ref, base_ref,
    ids_v, table_v, table_s, src, first_pool, current, staged_one, staged_two, *rest,
):
    f32, bf16 = jnp.float32, jnp.bfloat16
    rings = (rest[:14], rest[14:42])
    sems = (rest[42:48], rest[48:54])
    ids_s, ids_r, table_sem = rest[54:]
    x, y, z, c = my_place()
    near = lax.rem(y, 2)
    far_y, far_c = y + 1 - 2 * near, 1 - c
    me = z * 4 + near * 2 + c
    turn = (place(x, y, lax.rem(z + 1, 8), c), place(x, y, lax.rem(z + 7, 8), c))
    sides = (
        (place(x, far_y, z, c), z * 4 + (1 - near) * 2 + c),
        (place(x, far_y, z, far_c), z * 4 + (1 - near) * 2 + far_c),
        (place(x, y, z, far_c), z * 4 + near * 2 + far_c),
    )

    def remote(from_ref, to_ref, send_sem, recv_sem, target):
        return pltpu.make_async_remote_copy(
            src_ref=from_ref, dst_ref=to_ref, send_sem=send_sem, recv_sem=recv_sem,
            device_id=target, device_id_type=MESH,
        )

    barrier = pltpu.get_barrier_semaphore()
    for d in range(1, 8):
        pl.semaphore_signal(
            barrier, inc=1, device_id=place(x, y, lax.rem(z + d, 8), c), device_id_type=MESH
        )
    for target, _ in sides:
        pl.semaphore_signal(barrier, inc=1, device_id=target, device_id_type=MESH)

    ids_v[...] = jnp.zeros_like(ids_v)
    ids_v[0:1, 0:32] = ids_ref[...]
    masks = mask_ref[...].astype(f32)
    for q in range(2):
        for t in range(4):
            begin = t * 128 + q * 64
            src[q, t, 0:64] = feat_ref[begin : begin + 64]
            pair = masks[2 * q : 2 * q + 2, t * 128 : (t + 1) * 128]
            src[q, t, 64:72] = jnp.concatenate([pair, jnp.zeros((6, 128), f32)], 0).astype(bf16)
            first_pool[32 + t, q] = src[q, t]
    pl.semaphore_wait(barrier, 10)

    def ids_copy(d):
        return remote(
            ids_v, table_v.at[z], ids_s.at[d - 1], ids_r.at[d - 1],
            place(x, y, lax.rem(z + d, 8), c),
        )

    def learn_ids():
        table_v[z] = ids_v[...]
        for d in range(1, 8):
            ids_copy(d).wait_recv()
        local = pltpu.make_async_copy(table_v, table_s, table_sem)
        local.start()
        local.wait()

    def swap(chunks, src_ref, out, staged, ring, marks, ready, before_others):
        lane_s, lane_r = marks[0:2], marks[2:4]
        side_s, side_r = marks[4:6]
        half = chunks // 2

        def held(lane, step, q):
            return ring[6 * chunks + q] if step == 4 else ring[(lane * 3 + step - 1) * chunks + q]

        def along(lane, step, q):
            block = src_ref.at[q] if step == 0 else held(lane, step, q)
            return remote(
                block, held(lane, step + 1, q), lane_s[lane].at[step, q],
                lane_r[lane].at[step, q], turn[lane],
            )

        def carried(lane, step, q):
            return step < 3 or (q < half if lane == 0 else q >= half)

        def side_copy(i, k, q, source):
            return remote(
                staged.at[i, k, q], out.at[source * 4 + near * 2 + c, q],
                side_s.at[i, k], side_r.at[i, k], sides[k][0],
            )

        def deliver(i, source, block, q, ids):
            for k in range(3):
                staged[i, k, q] = block(ids(sides[k][1]))
            out[source * 4 + near * 2 + c, q] = block(ids(me))
            for k in range(3):
                side_copy(i, k, q, source).start()

        for q in range(chunks):
            ready(q)
            for lane in range(2):
                along(lane, 0, q).start()
            deliver(0, z, lambda t: src_ref[q, t], q, lambda to: own_ids[to])
        before_others()
        for step in range(1, 4):
            for q in range(chunks):
                for lane in range(2):
                    along(lane, step - 1, q).wait_recv()
                    if carried(lane, step, q):
                        along(lane, step, q).start()
                for lane in range(2):
                    source = lax.rem(z + (8 - step if lane == 0 else step), 8)
                    block = held(lane, step, q)
                    deliver(
                        1 + lane * 3 + step - 1, source, lambda t: block[t], q,
                        lambda to: table_s[source, 0, to],
                    )
        source = lax.rem(z + 4, 8)
        for n in range(half):
            for lane in range(2):
                q = n + lane * half
                along(lane, 3, q).wait_recv()
                block = held(0, 4, q)
                deliver(7, source, lambda t: block[t], q, lambda to: table_s[source, 0, to])
        for i in range(8):
            for k in range(3):
                remote(
                    staged.at[i, k], out.at[i], side_s.at[i, k], side_r.at[i, k], sides[k][0]
                ).wait_recv()

        def finish():
            for step in range(4):
                for q in range(chunks):
                    for lane in range(2):
                        if carried(lane, step, q):
                            along(lane, step, q).wait_send()
            for i in range(8):
                for k in range(3):
                    remote(
                        staged.at[i, k], out.at[i], side_s.at[i, k], side_r.at[i, k], sides[k][0]
                    ).wait_send()

        return finish

    for d in range(1, 8):
        ids_copy(d).start()
    finish_one = swap(
        2, src, first_pool, staged_one, rings[0], sems[0], lambda q: None, learn_ids
    )

    eye = jnp.where(
        lax.broadcasted_iota(jnp.int32, (128, 128), 0)
        == lax.broadcasted_iota(jnp.int32, (128, 128), 1),
        1.0, 0.0,
    ).astype(bf16)

    def first_hop(s):
        def tile_and_mask(slot):
            tile = jnp.concatenate([first_pool[slot, 0, 0:64], first_pool[slot, 1, 0:64]], 0)
            row = 64 + s % 2
            return tile, first_pool[slot, s // 2, row : row + 1]

        def row_tile(r, carry):
            own, mask = tile_and_mask(32 + r)
            masked = jnp.dot(eye * mask, own, preferred_element_type=f32)
            result = jnp.zeros((128, 128), f32)
            for j in range(0, 10, 2):
                blocks, tiles = [], []
                for i in range(2):
                    tile, mask = tile_and_mask(slots_ref[r, j + i])
                    blocks.append(adj_ref[r, j + i] * mask)
                    tiles.append(tile)
                result += jnp.dot(
                    jnp.concatenate(blocks, 1), jnp.concatenate(tiles, 0),
                    preferred_element_type=f32,
                )
            current[s, r] = result.astype(bf16)
            base_ref[r, s] = masked + result
            return carry

        lax.fori_loop(0, 4, row_tile, 0)

    def own_tiles():
        for q in range(4):
            for t in range(4):
                pool_ref[32 + t, q] = current[q, t]

    finish_two = swap(
        4, current, pool_ref, staged_two, rings[1], sems[1], first_hop, own_tiles
    )
    for d in range(1, 8):
        ids_copy(d).wait_send()
    finish_one()
    finish_two()


def spread(own_ids, slots, features, masks, adj):
    bf16, f32, i32 = jnp.bfloat16, jnp.float32, jnp.int32
    dma = pltpu.SemaphoreType.DMA
    vmem = pl.BlockSpec(memory_space=pltpu.VMEM)
    smem = pl.BlockSpec(memory_space=pltpu.SMEM)

    def marks(chunks):
        return [dma((4, chunks))] * 4 + [dma((8, 3))] * 2

    return pl.pallas_call(
        spread_kernel,
        name="spread",
        out_shape=(
            jax.ShapeDtypeStruct((36, 4, 128, 128), bf16),
            jax.ShapeDtypeStruct((4, 4, 128, 128), f32),
        ),
        in_specs=[smem, smem] + [vmem] * 4,
        out_specs=(vmem, vmem),
        scratch_shapes=[
            pltpu.VMEM((8, 128), i32),
            pltpu.VMEM((8, 8, 128), i32),
            pltpu.SMEM((8, 8, 128), i32),
            pltpu.VMEM((2, 4, 72, 128), bf16),
            pltpu.VMEM((36, 2, 72, 128), bf16),
            pltpu.VMEM((4, 4, 128, 128), bf16),
            pltpu.VMEM((8, 3, 2, 72, 128), bf16),
            pltpu.VMEM((8, 3, 4, 128, 128), bf16),
        ]
        + [pltpu.VMEM((4, 72, 128), bf16)] * 14
        + [pltpu.VMEM((4, 128, 128), bf16)] * 28
        + marks(2)
        + marks(4)
        + [dma((7,)), dma((7,)), dma(())],
        compiler_params=pltpu.CompilerParams(collective_id=1, has_side_effects=True),
    )(own_ids, slots, own_ids[None], features, masks, adj)


def column(row):
    return jnp.broadcast_to(row, (128, 128)).T[:, :1]


def learn_kernel(
    slots_ref, adj_ref, pool_ref, base_ref, labels_ref, labeled_ref,
    w_in_ref, b_in_ref, w_out_ref, b_out_ref, o_ref,
    xbar, xbar_t, pre_s, act, slope, prob_s, dlog, dlog_t, dpre_s, g_ref,
    core_in, held, first_in, second, second_in, third, third_in, fourth,
    core_s, core_r, one_s, one_r, two_s, two_r, three_s, three_r,
    four_s, four_r, five_s, five_r, six_s, six_r,
):
    f32, bf16 = jnp.float32, jnp.bfloat16
    classes = w_out_ref.shape[0]
    nt = (((1,), (1,)), ((), ()))
    x, y, z, c = my_place()
    other = lax.rem(c + 1, 2)
    partner = place(x, y, z, other)
    mine = (z, y)

    def along(axis, d):
        if axis == 0:
            k = lax.rem(z + d, 8)
            return k, place(x, y, k, c)
        k = lax.rem(y + d, 8)
        return k, place(x, k, z, c)

    def remote(src, dst, send_sem, recv_sem, target):
        return pltpu.make_async_remote_copy(
            src_ref=src, dst_ref=dst, send_sem=send_sem, recv_sem=recv_sem,
            device_id=target, device_id_type=MESH,
        )

    def each(start, stop, body):
        def step(i, carry):
            body(i)
            return carry

        lax.fori_loop(start, stop, step, 0)

    barrier = pltpu.get_barrier_semaphore()
    pl.semaphore_signal(barrier, inc=1, device_id=partner, device_id_type=MESH)

    def greet(d):
        for axis in range(2):
            pl.semaphore_signal(barrier, inc=1, device_id=along(axis, d)[1], device_id_type=MESH)

    def greet_x(d):
        target = place(lax.rem(x + d, 4), y, z, c)
        pl.semaphore_signal(barrier, inc=1, device_id=target, device_id_type=MESH)

    each(1, 8, greet)
    each(1, 4, greet_x)
    second[...] = jnp.zeros_like(second)
    g_ref[...] = jnp.zeros_like(g_ref)

    def row_tile(r, bias_total):
        hop = jnp.zeros((128, 512), f32)
        for j in range(0, 10, 2):
            lhs = jnp.concatenate([adj_ref[r, j], adj_ref[r, j + 1]], 1)
            rhs = jnp.concatenate(
                [
                    jnp.concatenate([pool_ref[slots_ref[r, j + i], s] for s in range(4)], 1)
                    for i in range(2)
                ],
                0,
            )
            hop += jnp.dot(lhs, rhs, preferred_element_type=f32)
        for s in range(4):
            mean = (base_ref[r, s] + hop[:, s * 128 : (s + 1) * 128]) * (
                1.0 / ((ORDER + 1) * KEEP_RATE)
            )
            at = pl.ds(pl.multiple_of(r * 512 + s * 128, 128), 128)
            xbar[s * 128 : (s + 1) * 128] = mean.astype(bf16)
            xbar_t[:, at] = mean.T.astype(bf16)

        for h in range(4):
            cols = slice(h * 256, (h + 1) * 256)
            pre_s[h] = (
                jnp.dot(xbar[...], w_in_ref[:, cols], preferred_element_type=f32)
                + b_in_ref[:, cols]
            )
            for b in range(0, 512, 32):
                at = pl.ds(pl.multiple_of(r * 512 + b, 32), 32)
                pre = pre_s[h, b : b + 32]
                sigma = 0.5 * jnp.tanh(0.5 * pre) + 0.5
                value = pre * sigma
                act[h, at] = value.astype(bf16)
                slope[h, at] = sigma + value * (1.0 - sigma)

        here = pl.ds(pl.multiple_of(r * 512, 512), 512)
        hidden = jnp.concatenate([act[h, here] for h in range(4)], 1)
        prob_s[...] = (
            lax.dot_general(hidden, w_out_ref[...], nt, preferred_element_type=f32) + b_out_ref[...]
        )
        average = jnp.zeros((128, classes), f32)
        for s in range(4):
            expo = jnp.exp(prob_s[s * 128 : (s + 1) * 128])
            part = expo * (1.0 / jnp.sum(expo, -1, keepdims=True))
            prob_s[s * 128 : (s + 1) * 128] = part
            average = average + part
        average = average * 0.25
        squares = average * average
        sharp = squares * (1.0 / jnp.sum(squares, -1, keepdims=True))
        label = column(labels_ref[pl.ds(r, 1), :].astype(f32)).astype(jnp.int32)
        used = column(labeled_ref[pl.ds(r, 1), :].astype(f32))
        onehot = (label == lax.broadcasted_iota(jnp.int32, (128, classes), 1)).astype(f32)
        for s in range(4):
            part = prob_s[s * 128 : (s + 1) * 128]
            push = 2.0 * (part - sharp)
            inner = jnp.sum(push * part, -1, keepdims=True)
            dlogits = (used * (part - onehot) + part * (push - inner)) * (1.0 / 2048.0)
            bias_total = bias_total + jnp.sum(dlogits, 0, keepdims=True)
            at = pl.ds(pl.multiple_of(r * 512 + s * 128, 128), 128)
            dlog[at] = dlogits.astype(bf16)
            dlog_t[:, at] = dlogits.T.astype(bf16)
        return bias_total

    bias_total = lax.fori_loop(0, 4, row_tile, jnp.zeros((1, classes), f32))
    g_ref[0, 301:302, :] = bias_total[:, :128]
    g_ref[1, 301:302, : classes - 128] = bias_total[:, 128:]

    def chunk(h):
        cols = pl.ds(pl.multiple_of(h * 256, 256), 256)

        def back(r, total):
            here = pl.ds(pl.multiple_of(r * 512, 512), 512)
            dact = jnp.dot(dlog[here], w_out_ref[:, cols], preferred_element_type=f32)
            dpre = dact * slope[h, here]
            dpre_s[here] = dpre.astype(bf16)
            return total + jnp.sum(dpre.reshape(64, 8, 256), 0)

        total = lax.fori_loop(0, 4, back, jnp.zeros((8, 256), f32))
        b_in_grad = jnp.sum(total, 0, keepdims=True)
        w_in_grad = jnp.dot(xbar_t[...], dpre_s[...], preferred_element_type=f32)
        w_out_grad = jnp.dot(dlog_t[...], act[h], preferred_element_type=f32)
        for i in range(2):
            lanes = slice(i * 128, (i + 1) * 128)
            g_ref[2 * h + i, :128] = w_in_grad[:, lanes]
            g_ref[2 * h + i, 128 : 128 + classes] = w_out_grad[:, lanes]
            g_ref[2 * h + i, 300:301] = b_in_grad[:, lanes]

    def piece_at(core, half, k):
        row = pl.ds(pl.multiple_of(lax.rem(k, 4) * 80, 16), 80)
        return core * 4 + half * 2 + lax.div(k, 4), row

    def core_copy(half, d):
        k = lax.rem(mine[half] + d, 8)
        return remote(
            g_ref.at[piece_at(other, half, k)], core_in.at[half, k],
            core_s.at[half, d], core_r.at[half, d], partner,
        )

    for half in range(2):
        chunk(other * 2 + half)
        if half == 0:
            pl.semaphore_wait(barrier, 18)
        each(1, 9, lambda i: core_copy(half, lax.rem(i, 8)).start())

    def one_copy(half, d):
        k, target = along(half, d)
        return remote(
            held.at[half, k], first_in.at[half, d - 1],
            one_s.at[half, d - 1], one_r.at[half, d - 1], target,
        )

    for half in range(2):
        chunk(c * 2 + half)

        def core_add(i):
            d = lax.rem(i, 8)
            k = lax.rem(mine[half] + d, 8)
            core_copy(half, d).wait_recv()
            held[half, k] = (g_ref[piece_at(c, half, k)] + core_in[half, k]).reshape(5, 16, 128)

        def one_step(d):
            core_add(d)
            one_copy(half, d).start()

        each(1, 8, one_step)
        core_add(8)

    for half in range(2):
        each(1, 8, lambda d: one_copy(half, d).wait_recv())
        total = held[half, mine[half]]
        for d in range(7):
            total = total + first_in[half, d]
        second[half, pl.ds(0, 5)] = total

    def two_copy(half, d):
        k, target = along(1 - half, d)
        return remote(
            second.at[half, k], second_in.at[half, d - 1],
            two_s.at[half, d - 1], two_r.at[half, d - 1], target,
        )

    def two_step(d):
        for half in range(2):
            two_copy(half, d).start()

    def two_wait(d):
        for half in range(2):
            two_copy(half, d).wait_recv()

    each(1, 8, two_step)
    each(1, 8, two_wait)
    for half in range(2):
        total = second[half, mine[1 - half]]
        for d in range(7):
            total = total + second_in[half, d]
        third[half] = total

    def three_copy(d):
        target = place(lax.rem(x + d, 4), y, z, c)
        return remote(third, third_in.at[x], three_s.at[d - 1], three_r.at[d - 1], target)

    each(1, 4, lambda d: three_copy(d).start())
    third_in[x] = third[...]
    each(1, 4, lambda d: three_copy(d).wait_recv())
    total = (third_in[0] + third_in[1]) + (third_in[2] + third_in[3])
    for half in range(2):
        fourth[half, mine[1 - half]] = total[half]

    def four_copy(half, d):
        target = along(1 - half, d)[1]
        piece = fourth.at[half, mine[1 - half]]
        return remote(piece, piece, four_s.at[half, d - 1], four_r.at[half, d - 1], target)

    def four_step(d):
        for half in range(2):
            four_copy(half, d).start()

    def four_wait(d):
        for half in range(2):
            four_copy(half, d).wait_recv()

    each(1, 8, four_step)
    each(1, 8, four_wait)

    def five_copy(half, d):
        target = along(half, d)[1]
        return remote(
            fourth.at[half, pl.ds(0, 5)], o_ref.at[c, half, mine[half]],
            five_s.at[half, d - 1], five_r.at[half, d - 1], target,
        )

    def five_step(d):
        for half in range(2):
            five_copy(half, d).start()

    each(1, 8, five_step)

    def six_copy(half, d):
        k = lax.rem(mine[half] + 8 - d, 8)
        piece = o_ref.at[c, half, k]
        return remote(piece, piece, six_s.at[half, d - 1], six_r.at[half, d - 1], partner)

    def six_own(half):
        return remote(
            fourth.at[half, pl.ds(0, 5)], o_ref.at[c, half, mine[half]],
            six_s.at[half, 7], six_r.at[half, 7], partner,
        )

    for half in range(2):
        six_own(half).start()
        o_ref[c, half, mine[half]] = fourth[half, pl.ds(0, 5)]

    def six_step(d):
        for half in range(2):
            five_copy(half, d).wait_recv()
            six_copy(half, d).start()

    each(1, 8, six_step)

    def finish(d):
        for half in range(2):
            one_copy(half, d).wait_send()
            two_copy(half, d).wait_send()
            four_copy(half, d).wait_send()
            five_copy(half, d).wait_send()
            six_copy(half, d).wait_send()
            six_copy(half, d).wait_recv()

    def finish_core(d):
        for half in range(2):
            core_copy(half, d).wait_send()

    each(1, 8, finish)
    each(0, 8, finish_core)
    each(1, 4, lambda d: three_copy(d).wait_send())
    for half in range(2):
        six_own(half).wait_send()
        six_own(half).wait_recv()


def learn(slots, adj, pool, base, labels, labeled, w_in, b_in, w_out_t, b_out):
    vmem = pl.BlockSpec(memory_space=pltpu.VMEM)
    classes = w_out_t.shape[0]
    bf16, f32 = jnp.bfloat16, jnp.float32
    piece = (5, 16, 128)
    dma = pltpu.SemaphoreType.DMA
    return pl.pallas_call(
        learn_kernel,
        name="learn",
        out_shape=jax.ShapeDtypeStruct((2, 2, 8) + piece, f32),
        in_specs=[pl.BlockSpec(memory_space=pltpu.SMEM)] + [vmem] * 9,
        out_specs=vmem,
        scratch_shapes=[
            pltpu.VMEM((512, 128), bf16),
            pltpu.VMEM((128, 2048), bf16),
            pltpu.VMEM((4, 512, 256), f32),
            pltpu.VMEM((4, 2048, 256), bf16),
            pltpu.VMEM((4, 2048, 256), f32),
            pltpu.VMEM((512, classes), f32),
            pltpu.VMEM((2048, classes), bf16),
            pltpu.VMEM((classes, 2048), bf16),
            pltpu.VMEM((2048, 256), bf16),
            pltpu.VMEM((8, GROWS, 128), f32),
            pltpu.VMEM((2, 8, 80, 128), f32),
            pltpu.VMEM((2, 8) + piece, f32),
            pltpu.VMEM((2, 7) + piece, f32),
            pltpu.VMEM((2, 8, 16, 128), f32),
            pltpu.VMEM((2, 7, 16, 128), f32),
            pltpu.VMEM((2, 16, 128), f32),
            pltpu.VMEM((4, 2, 16, 128), f32),
            pltpu.VMEM((2, 8, 16, 128), f32),
        ]
        + [dma((2, 8))] * 2
        + [dma((2, 7))] * 4
        + [dma((3,))] * 2
        + [dma((2, 7))] * 4
        + [dma((2, 8))] * 2,
        compiler_params=pltpu.CompilerParams(collective_id=0, has_side_effects=True),
    )(slots, adj, pool, base, labels, labeled, w_in, b_in, w_out_t, b_out)


def unpack_kernel(g_ref, w_in_ref, b_in_ref, w_out_ref, b_out_ref):
    classes = w_out_ref.shape[0]
    for i in range(8):
        lanes = slice(i * 128, (i + 1) * 128)
        w_in_ref[:, lanes] = g_ref[i, :128]
        w_out_ref[:, lanes] = g_ref[i, 128 : 128 + classes]
        b_in_ref[:, lanes] = g_ref[i, 300:301]
    b_out_ref[:, :128] = g_ref[0, 301:302]
    b_out_ref[:, 128:] = g_ref[1, 301:302, : classes - 128]


def unpack(summed, classes):
    vmem = pl.BlockSpec(memory_space=pltpu.VMEM)
    shapes = ((128, 1024), (1, 1024), (classes, 1024), (1, classes))
    return pl.pallas_call(
        unpack_kernel,
        name="unpack",
        out_shape=tuple(jax.ShapeDtypeStruct(s, jnp.float32) for s in shapes),
        in_specs=[vmem],
        out_specs=(vmem,) * 4,
    )(summed)


def per_device(
    features, keep_masks, serve_ids, col_slot, adj_blocks, node_labels, labeled,
    weight_in, bias_in, weight_out, bias_out,
):
    classes = weight_out.shape[1]
    slots, adj = col_slot[0], adj_blocks[0]
    pool, base = spread(serve_ids.reshape(-1), slots, features[0], keep_masks[0], adj)
    summed = learn(
        slots, adj, pool, base, node_labels.reshape(4, 128), labeled.reshape(4, 128),
        weight_in, bias_in[None], weight_out.T, bias_out[None],
    )
    w_in, b_in, w_out_t, b_out = unpack(summed.reshape(8, GROWS, 128), classes)
    return (w_in, b_in[0], w_out_t.T, b_out[0])


def solution(mesh):
    placed = (
        P("dp", "dom", None),
        P("dp", None, "dom"),
        P("dp", "dom", None, None),
        P("dp", "dom", None),
        P("dp", "dom", None, None, None),
        P("dp", "dom"),
        P("dp", "dom"),
        P(),
        P(),
        P(),
        P(),
    )
    return jax.shard_map(
        per_device, mesh=mesh, in_specs=placed, out_specs=(P(), P(), P(), P()), check_vma=False
    )
```
